768 devices in a mesh: blk: 96 (over y, z_lo, x), rep: 8 (over z_hi, core).
Axes of the slice: x: 4, y: 8, z: 12 (z_hi: 4, z_lo: 3; z = z_hi * 3 + z_lo), core: 2. Of those that a mesh axis runs over, the one named last changes fastest.
Arguments:
- features: bfloat16 [49152, 512], P('blk'), may hold values from -2000 to 2000
- labels: int32 [49152], P('blk'), may hold values from 0 to 127
- w_first: bfloat16 [512, 512], replicated, may hold values from -0.25 to 0.25
- w_second: bfloat16 [512, 128], replicated, may hold values from -0.25 to 0.25
- block_rows: int32 [96, 8, 12, 2], P('blk', 'rep'), may hold values from 0 to 1, as said below
- block_cols: int32 [96, 8, 12, 2], P('blk', 'rep'), may hold values from 0 to 1
- block_vals: bfloat16 [96, 8, 12, 2, 256, 256], P('blk', 'rep')
Outputs:
- logits: bfloat16 [49152, 128], P('blk')
- grad_first: float32 [512, 512], replicated
- grad_second: float32 [512, 128], replicated
- loss: float32 [], replicated
The draws below stay inside these ranges and needn't reach their ends.
Inputs may be any that keep to these rules, and one draw needn't show every extreme that they name: `block_rows`: slot (i, r, t, p) holds a block of shard i's rows against shard (i - r * 12 - t) mod 96's columns; the matrix A assembled from all slots is symmetric; slots whose values are all zero are padding.
All inputs are finite; a program needn't handle non-finite values.
Results may differ from the reference program's by a relative error of at most 0.0083.
Values may be sent and summed in bfloat16 or wider, within the bound.
No kernel may reach another device: no remote copies, remote signals or barrier semaphores. Data moves between devices by JAX's collectives and lax.ppermute only.
A program may use at most 32 MiB of HBM per device.

```python
import math
import jax
import jax.numpy as jnp
from jax import lax

C = 128
F = 512
HID = 512
BS = 256
RB = 2
HOPS = 2
PC = 2
SHARDS = 96
REPS = 8
STEPS_DEV = 12
NODES = 49152
GB = 192


def layout(key):
    full = (SHARDS, REPS, STEPS_DEV, PC)
    shard = jnp.broadcast_to(jnp.arange(SHARDS, dtype=jnp.int32)[:, None, None, None], full)
    repl = jnp.broadcast_to(jnp.arange(REPS, dtype=jnp.int32)[None, :, None, None], full)
    stepn = jnp.broadcast_to(jnp.arange(STEPS_DEV, dtype=jnp.int32)[None, None, :, None], full)
    slot = jnp.broadcast_to(jnp.arange(PC, dtype=jnp.int32)[None, None, None, :], full)
    other = (shard - repl * STEPS_DEV - stepn) % SHARDS
    lower = jnp.minimum(shard, other)
    upper = jnp.maximum(shard, other)
    picks = jax.random.randint(jax.random.fold_in(key, 11), (SHARDS, SHARDS, PC), 0, RB)
    live_tab = jax.random.randint(jax.random.fold_in(key, 12), (SHARDS, SHARDS), 0, 4)
    flip_tab = jax.random.randint(jax.random.fold_in(key, 13), (SHARDS,), 0, 2)
    chosen = picks[lower, upper, slot]
    flip = flip_tab[shard]
    diag_cols = jnp.where(flip == 1, slot, RB - 1 - slot)
    rows = jnp.where(shard > other, chosen, slot)
    cols = jnp.where(shard < other, chosen, jnp.where(shard > other, slot, diag_cols))
    live = live_tab[lower, upper] > 0
    return (rows.astype(jnp.int32), cols.astype(jnp.int32), other, live)


def draw_block_rows(key, part):
    rows, cols, other, live = layout(key)
    return rows


def draw_block_cols(key, part):
    rows, cols, other, live = layout(key)
    return cols


def draw_block_vals(key, part):
    rows, cols, other, live = layout(key)
    shard = jnp.broadcast_to(jnp.arange(SHARDS, dtype=jnp.int32)[:, None, None, None], rows.shape)
    grow = shard * RB + rows
    gcol = other * RB + cols
    pair = jnp.minimum(grow, gcol) * GB + jnp.maximum(grow, gcol)
    value_key = jax.random.fold_in(key, 21)
    scale = 1.0 / math.sqrt(SHARDS * BS)

    def one_shard(index):
        pid = pair[index].reshape(-1)
        gr = grow[index].reshape(-1)
        gc = gcol[index].reshape(-1)
        alive = live[index].reshape(-1)
        keys = jax.vmap(lambda p: jax.random.fold_in(value_key, p))(pid)
        blocks = jax.vmap(lambda k: jax.random.normal(k, (BS, BS), jnp.float32))(keys)
        flipped = jnp.swapaxes(blocks, 1, 2)
        sym = (blocks + flipped) * math.sqrt(0.5)
        chosen = jnp.where((gr < gc)[:, None, None], blocks, jnp.where((gr > gc)[:, None, None], flipped, sym))
        chosen = chosen * scale * alive.astype(jnp.float32)[:, None, None]
        return chosen.astype(jnp.bfloat16).reshape(REPS, STEPS_DEV, PC, BS, BS)
    return lax.map(one_shard, jnp.arange(SHARDS, dtype=jnp.int32))


def draw_features(key, part):
    values = jax.random.truncated_normal(jax.random.fold_in(key, 1), -6.0, 6.0, (NODES, F), jnp.float32)
    return values.astype(jnp.bfloat16)


def touch_ends(values, stream_key, least, top_value):
    longest = values.shape.index(max(values.shape))
    spots = []
    for shift in (0, 1):
        where = [jax.random.randint(jax.random.fold_in(stream_key, axis), (), 0, length) for axis, length in enumerate(values.shape)]
        where[longest] = (where[longest] + shift) % values.shape[longest]
        spots.append(tuple(where))
    return values.at[spots[0]].set(least).at[spots[1]].set(top_value)


def normal_values(stream_key, dims, scale, reach, kind=jnp.bfloat16):
    result = scale * jax.random.normal(stream_key, dims, jnp.float32)
    return jnp.clip(result, min=-reach, max=reach).astype(kind)


def setup_inputs(seed: int = 0) -> dict:
    key_list = jax.random.split(jax.random.key(seed), 8)
    features = draw_features(jax.random.fold_in(key_list[7], 71), 0)
    labels = touch_ends(jax.random.randint(key_list[1], (NODES,), 0, C), jax.random.fold_in(key_list[1], 1), 0, C - 1).astype(jnp.int32)
    w_first = normal_values(key_list[2], (F, HID), F ** -0.5, 0.25)
    w_second = normal_values(key_list[3], (HID, C), HID ** -0.5, 0.25)
    block_rows = draw_block_rows(jax.random.fold_in(key_list[7], 71), 0)
    block_cols = draw_block_cols(jax.random.fold_in(key_list[7], 71), 0)
    block_vals = draw_block_vals(jax.random.fold_in(key_list[7], 71), 0)
    return dict(features=features, labels=labels, w_first=w_first, w_second=w_second, block_rows=block_rows, block_cols=block_cols, block_vals=block_vals)


alpha_rate = 0.1

def propagate(panel, block_rows, block_cols, block_vals):
    tiles = panel.reshape(SHARDS * RB, BS, C)
    offsets = jnp.arange(REPS, dtype=jnp.int32)[:, None] * STEPS_DEV + jnp.arange(STEPS_DEV, dtype=jnp.int32)[None, :]

    def one_shard(carry, shard):
        rows = block_rows[shard].reshape(-1)
        cols = block_cols[shard].reshape(-1)
        other = jnp.broadcast_to(((shard - offsets) % SHARDS)[:, :, None], (REPS, STEPS_DEV, PC)).reshape(-1)
        picked = tiles[other * RB + cols]
        blocks = block_vals[shard].reshape(-1, BS, BS)
        prods = jnp.einsum('nab,nbc->nac', blocks.astype(jnp.float32), picked.astype(jnp.float32))
        summed = jax.ops.segment_sum(prods, rows, num_segments=RB)
        return (carry, summed)
    _, outs = lax.scan(one_shard, jnp.zeros((), jnp.int32), jnp.arange(SHARDS, dtype=jnp.int32))
    return outs.reshape(NODES, C)

def reference(features, labels, w_first, w_second, block_rows, block_cols, block_vals):
    hidden = jax.nn.relu(jnp.dot(features, w_first, preferred_element_type=jnp.float32)).astype(jnp.bfloat16)
    base = jnp.dot(hidden, w_second, preferred_element_type=jnp.float32).astype(jnp.bfloat16)
    base32 = base.astype(jnp.float32)
    current = base
    for step in range(HOPS):
        mixed = (1.0 - alpha_rate) * propagate(current, block_rows, block_cols, block_vals) + alpha_rate * base32
        current = mixed.astype(jnp.bfloat16)
    logits = mixed.astype(jnp.bfloat16)
    onehot = (labels[:, None] == jnp.arange(C, dtype=jnp.int32)[None, :]).astype(jnp.float32)
    lse = jax.nn.logsumexp(mixed, axis=1)
    picked = lax.optimization_barrier(jnp.sum(mixed * onehot, axis=1))
    loss = jnp.mean(lse - picked)
    scale = 1.0 / jnp.sqrt(jnp.float32(NODES))
    grad_out = (jax.nn.softmax(mixed, axis=1) - onehot) * scale
    grad_base = alpha_rate * grad_out
    moving = grad_out.astype(jnp.bfloat16)
    for step in range(HOPS):
        nxt = (1.0 - alpha_rate) * propagate(moving, block_rows, block_cols, block_vals)
        if step + 1 < HOPS:
            grad_base = grad_base + alpha_rate * nxt
            moving = nxt.astype(jnp.bfloat16)
        else:
            grad_base = grad_base + nxt
    grad_b = grad_base.astype(jnp.bfloat16)
    grad_second = jnp.dot(hidden.T, grad_b, preferred_element_type=jnp.float32)
    back = jnp.dot(grad_b, w_second.T, preferred_element_type=jnp.float32)
    grad_hidden = jnp.where(hidden > 0, back, 0.0).astype(jnp.bfloat16)
    grad_first = jnp.dot(features.T, grad_hidden, preferred_element_type=jnp.float32)
    return (logits, grad_first, grad_second, loss)
```

```python
import functools
import math

import jax
import jax.numpy as jnp
from jax import lax
from jax.experimental import pallas as pl
from jax.experimental.pallas import tpu as pltpu
from jax.sharding import Mesh
from jax.sharding import PartitionSpec as P

ALPHA = 0.1
BF = jnp.bfloat16
F32 = jnp.float32
REP = ("zh", "c")
BLK = ("y", "q")


def scatter_kernel(index_ref, tiles_ref, panel_ref, out_ref):
    steps, slots, width, _ = tiles_ref.shape
    blocks = out_ref.shape[1] // width
    q = index_ref[2 * steps * slots]
    share = jnp.where(index_ref[2 * steps * slots + 1] == 1, ALPHA / (1.0 - ALPHA), 0.0).astype(F32)
    for t in range(steps):
        place = lax.rem(q + (steps - t), steps)
        products = []
        for p in range(slots):
            row = index_ref[t * slots + p]
            piece = panel_ref[pl.ds(pl.multiple_of(row * width, width), width), :]
            products.append(
                lax.dot_general(
                    tiles_ref[t, p], piece, (((0,), (0,)), ((), ())), preferred_element_type=F32
                )
            )
        for b in range(blocks):
            total = jnp.zeros(products[0].shape, F32)
            for p in range(slots):
                col = index_ref[steps * slots + t * slots + p]
                total = total + jnp.where(col == b, products[p], 0.0)
            if t == 0:
                total = total + share * panel_ref[b * width : (b + 1) * width, :].astype(F32)
            out_ref[place, b * width : (b + 1) * width, :] = total.astype(BF)


def gather_kernel(index_ref, tiles_ref, panels_ref, out_ref):
    steps, slots, width, _ = tiles_ref.shape
    q = index_ref[2 * steps * slots]
    share = jnp.where(index_ref[2 * steps * slots + 1] == 1, ALPHA / (1.0 - ALPHA), 0.0).astype(F32)
    out_ref[...] = share * panels_ref[q].astype(F32)
    for t in range(steps):
        place = lax.rem(q + (steps - t), steps)
        for p in range(slots):
            row = index_ref[t * slots + p]
            col = index_ref[steps * slots + t * slots + p]
            piece = panels_ref[place, pl.ds(pl.multiple_of(col * width, width), width), :]
            rows = pl.ds(pl.multiple_of(row * width, width), width)
            out_ref[rows, :] += jnp.dot(tiles_ref[t, p], piece, preferred_element_type=F32)


def call(kernel, shape, dtype, index, *operands, interpret=False):
    vmem = pl.BlockSpec(memory_space=pltpu.VMEM)
    return pl.pallas_call(
        kernel,
        out_shape=jax.ShapeDtypeStruct(shape, dtype),
        in_specs=[pl.BlockSpec(memory_space=pltpu.SMEM)] + [vmem] * len(operands),
        out_specs=vmem,
        interpret=interpret,
    )(index, *operands)


def on_device(interpret, features, labels, w_first, w_second, block_rows, block_cols, block_vals):
    nodes_here = features.shape[0]
    classes = w_second.shape[1]
    ny, nq, nzh, nc = (lax.axis_size(a) for a in ("y", "q", "zh", "c"))
    nrep = nzh * nc
    nblk = ny * nq
    q_id = lax.axis_index("q")
    c_id = lax.axis_index("c")
    rep_id = lax.axis_index(REP)
    nodes = nodes_here * nblk
    tiles = block_vals[0, 0]
    steps = tiles.shape[0]
    half = nodes_here // nc
    skewed = [[((y + r) % ny) * nrep + r for r in range(nrep)] for y in range(ny)]
    yrep = ("y",) + REP
    core_swap = [(i, (i + 1) % nc) for i in range(nc)]

    def index_of(flag):
        tail = jnp.stack([q_id, flag]).astype(jnp.int32)
        return jnp.concatenate([block_rows[0, 0].reshape(-1), block_cols[0, 0].reshape(-1), tail])

    plain = index_of(jnp.int32(0))
    diagonal = index_of((rep_id == 0).astype(jnp.int32))
    from_same = (jnp.arange(nq, dtype=jnp.int32) >= q_id)[:, None, None]

    def to_all(value, count):
        return jnp.broadcast_to(value[None], (count,) + value.shape)

    def with_transpose(panel, index):
        parts = call(
            scatter_kernel, (steps, nodes_here, classes), BF, index, tiles, panel, interpret=interpret
        )
        parts = lax.all_to_all(parts, "q", 0, 0, tiled=True).astype(F32)
        before = jnp.sum(jnp.where(from_same, 0.0, parts), axis=0).astype(BF)
        moved = lax.ppermute(before, "y", [((i + 1) % ny, i) for i in range(ny)])
        total = jnp.sum(jnp.where(from_same, parts, 0.0), axis=0) + moved.astype(F32)
        pieces = total.astype(BF).reshape(nrep, nodes_here // nrep, classes)
        pieces = lax.all_to_all(pieces, yrep, 0, 0, axis_index_groups=skewed, tiled=True)
        return (1.0 - ALPHA) * jnp.sum(pieces.astype(F32), axis=0)

    def with_plain(piece, index):
        here = lax.all_to_all(
            to_all(piece, nrep), yrep, 0, 0, axis_index_groups=skewed, tiled=True
        ).reshape(nodes_here, classes)
        before = lax.ppermute(here, "y", [(i, (i + 1) % ny) for i in range(ny)])
        panels = jnp.where(from_same, here[None], before[None])
        panels = lax.all_to_all(panels, "q", 0, 0, tiled=True)
        part = call(
            gather_kernel, (nodes_here, classes), F32, index, tiles, panels, interpret=interpret
        )
        away = lax.dynamic_slice_in_dim(part, (nc - 1 - c_id) * half, half, 0).astype(BF)
        mine = lax.dynamic_slice_in_dim(part, c_id * half, half, 0)
        chip = (mine + lax.ppermute(away, "c", core_swap).astype(F32)).astype(BF)
        chips = lax.all_to_all(to_all(chip, nzh), "zh", 0, 0, tiled=True)
        return (1.0 - ALPHA) * jnp.sum(chips.astype(F32), axis=0)

    def whole(mine):
        other = lax.ppermute(mine, "c", core_swap)
        return jnp.where(
            c_id == 0,
            jnp.concatenate([mine, other], axis=-2),
            jnp.concatenate([other, mine], axis=-2),
        )

    hidden = jax.nn.relu(jnp.dot(features, w_first, preferred_element_type=F32)).astype(BF)
    base = jnp.dot(hidden, w_second, preferred_element_type=F32).astype(BF)
    base_half = lax.dynamic_slice_in_dim(base, c_id * half, half, 0)

    current = with_transpose(base, diagonal).astype(BF)
    mixed = with_plain(current, plain) + ALPHA * base_half.astype(F32)
    labels_half = lax.dynamic_slice_in_dim(labels, c_id * half, half, 0)
    onehot = (labels_half[:, None] == jnp.arange(classes, dtype=jnp.int32)[None, :]).astype(F32)
    top = jnp.max(mixed, axis=1, keepdims=True)
    grown = jnp.exp(mixed - top)
    mass = jnp.sum(grown, axis=1, keepdims=True)
    picked = jnp.sum(mixed * onehot, axis=1, keepdims=True)
    ce_sum = jnp.sum(jnp.log(mass) + top - picked)
    grad_out = (grown / mass - onehot) * (1.0 / math.sqrt(nodes))
    both = whole(jnp.stack([grad_out.astype(BF), mixed.astype(BF)]))
    moving, logits = both[0], both[1]

    moving = with_transpose(moving, plain).astype(BF)
    grad_half = with_plain(moving, diagonal) + ALPHA * grad_out
    grad_b = whole(grad_half.astype(BF))

    part = hidden.shape[1] // nrep
    hidden_part = lax.dynamic_slice_in_dim(hidden, rep_id * part, part, 1)
    second_part = lax.dynamic_slice_in_dim(w_second, rep_id * part, part, 0)
    back = lax.dot_general(grad_b, second_part, (((1,), (1,)), ((), ())), preferred_element_type=F32)
    grad_hidden = jnp.where(hidden_part > 0, back, 0.0).astype(BF)
    first_rows = lax.dot_general(
        grad_hidden, features, (((0,), (0,)), ((), ())), preferred_element_type=F32
    )
    second_rows = lax.dot_general(
        hidden_part, grad_b, (((0,), (0,)), ((), ())), preferred_element_type=F32
    )
    width = features.shape[1]
    count_first = part * width // classes
    used = count_first + part
    each = -(-(used + 1) // nblk)
    loss_part = jnp.where(lax.axis_index("zh") == 0, ce_sum, 0.0)
    tail = jnp.zeros((each * nblk - used, classes), F32).at[0, 0].set(loss_part)
    sums = jnp.concatenate([first_rows.reshape(count_first, classes), second_rows, tail])
    sums = lax.all_to_all(sums.reshape(nblk, each, classes), BLK, 0, 0, tiled=True)
    sums = jnp.sum(sums, axis=0)
    lanes = lax.broadcasted_iota(jnp.int32, (each, classes), 1)
    rows = lax.broadcasted_iota(jnp.int32, (each, classes), 0)
    is_loss = (lax.axis_index(BLK) * each + rows) == used
    value = sums[used % each, 0]
    high = value.astype(BF).astype(F32)
    middle = (value - high).astype(BF).astype(F32)
    low = value - high - middle
    terms = jnp.where(lanes == 0, high, jnp.where(lanes == 1, middle, jnp.where(lanes == 2, low, 0.0)))
    sums = jnp.where(is_loss, terms, sums).astype(BF)
    sums = lax.all_to_all(to_all(sums, nrep), REP, 0, 0, tiled=True)
    sums = lax.all_to_all(to_all(sums, nblk), BLK, 0, 0, tiled=True)
    sums = jnp.swapaxes(sums.astype(F32), 0, 1).reshape(nrep, nblk * each, classes)
    grad_first = sums[:, :count_first].reshape(nrep * part, width).T
    grad_second = sums[:, count_first:used].reshape(nrep * part, classes)
    loss = jnp.sum(sums[:, used, :3]) / nodes
    return (logits, grad_first, grad_second, loss)


def solution(mesh, interpret=False):
    nblk, nrep = mesh.devices.shape
    cores = 2
    fine = Mesh(
        mesh.devices.reshape(nrep, nblk // nrep, nrep // cores, cores), ("y", "q", "zh", "c")
    )
    in_specs = (
        P(BLK, None),
        P(BLK),
        P(),
        P(),
        P(BLK, REP, None, None),
        P(BLK, REP, None, None),
        P(BLK, REP, None, None, None, None),
    )
    out_specs = (P(BLK, None), P(), P(), P())
    return jax.shard_map(
        functools.partial(on_device, interpret),
        mesh=fine,
        in_specs=in_specs,
        out_specs=out_specs,
        check_vma=False,
    )
```

```python
import functools
import math

import jax
import jax.numpy as jnp
from jax import lax
from jax.experimental import pallas as pl
from jax.experimental.pallas import tpu as pltpu
from jax.sharding import Mesh
from jax.sharding import PartitionSpec as P

ALPHA = 0.1
BF = jnp.bfloat16
F32 = jnp.float32
REP = ("zh", "c")
BLK = ("y", "q")


def scatter_kernel(place_ref, rows_ref, cols_ref, tiles_ref, panel_ref, out_ref):
    steps, slots, width, _ = tiles_ref.shape
    blocks = out_ref.shape[1] // width
    q = place_ref[0]
    share = jnp.where(place_ref[2] == 1, ALPHA / (1.0 - ALPHA), 0.0).astype(F32)
    for t in range(steps):
        place = lax.rem(q + (steps - t), steps)
        products = []
        for p in range(slots):
            rows = pl.ds(pl.multiple_of(rows_ref[p, t] * width, width), width)
            products.append(
                lax.dot_general(
                    tiles_ref[t, p],
                    panel_ref[rows, :],
                    (((0,), (0,)), ((), ())),
                    preferred_element_type=F32,
                )
            )
        for b in range(blocks):
            total = jnp.zeros(products[0].shape, F32)
            for p in range(slots):
                total = total + jnp.where(cols_ref[p, t] == b, products[p], 0.0)
            if t == 0:
                total = total + share * panel_ref[b * width : (b + 1) * width, :].astype(F32)
            out_ref[place, b * width : (b + 1) * width, :] = total.astype(BF)


def gather_kernel(
    place_ref, rows_ref, cols_ref, tiles_ref, panels_ref, mine_ref, away_ref, sum_ref
):
    steps, slots, width, _ = tiles_ref.shape
    half = mine_ref.shape[0]
    q = place_ref[0]
    c = place_ref[1]
    share = jnp.where(place_ref[2] == 1, ALPHA / (1.0 - ALPHA), 0.0).astype(F32)
    sum_ref[...] = share * panels_ref[q].astype(F32)
    for t in range(steps):
        place = lax.rem(q + (steps - t), steps)
        for p in range(slots):
            cols = pl.ds(pl.multiple_of(cols_ref[p, t] * width, width), width)
            rows = pl.ds(pl.multiple_of(rows_ref[p, t] * width, width), width)
            sum_ref[rows, :] += jnp.dot(
                tiles_ref[t, p], panels_ref[place, cols, :], preferred_element_type=F32
            )
    mine_ref[...] = sum_ref[pl.ds(pl.multiple_of(c * half, half), half), :]
    away_ref[...] = sum_ref[pl.ds(pl.multiple_of((1 - c) * half, half), half), :].astype(BF)


def call(kernel, outs, scalars, operands, scratch=(), interpret=False):
    vmem = pl.BlockSpec(memory_space=pltpu.VMEM)
    smem = pl.BlockSpec(memory_space=pltpu.SMEM)
    shapes = [jax.ShapeDtypeStruct(shape, dtype) for shape, dtype in outs]
    return pl.pallas_call(
        kernel,
        out_shape=shapes,
        in_specs=[smem] * len(scalars) + [vmem] * len(operands),
        out_specs=[vmem] * len(outs),
        scratch_shapes=list(scratch),
        interpret=interpret,
    )(*scalars, *operands)


def on_device(interpret, features, labels, w_first, w_second, block_rows, block_cols, block_vals):
    nodes_here = features.shape[0]
    classes = w_second.shape[1]
    ny, nq, nzh, nc = (lax.axis_size(a) for a in ("y", "q", "zh", "c"))
    nrep = nzh * nc
    nblk = ny * nq
    q_id = lax.axis_index("q")
    c_id = lax.axis_index("c")
    rep_id = lax.axis_index(REP)
    nodes = nodes_here * nblk
    tiles = block_vals[0, 0]
    steps = tiles.shape[0]
    half = nodes_here // nc
    yrep = ("y",) + REP
    fours = [
        [((y + zh * nc + c) % ny) * nrep + zh * nc + c for zh in range(nzh)]
        for y in range(ny)
        for c in range(nc)
    ]
    pairs = []
    for y in range(ny):
        for zh in range(nzh):
            here, there = y * nrep + zh * nc, ((y + 1) % ny) * nrep + zh * nc + 1
            pairs += [(here, there), (there, here)]
    cores = [(0, 1), (1, 0)]
    scalars = [block_rows[0, 0].T, block_cols[0, 0].T]

    def place(flag):
        return jnp.stack([q_id, c_id, flag]).astype(jnp.int32)

    plain = place(jnp.int32(0))
    diagonal = place((rep_id == 0).astype(jnp.int32))
    from_same = (jnp.arange(nq, dtype=jnp.int32) >= q_id)[:, None, None]

    def to_all(value, count):
        return jnp.broadcast_to(value[None], (count,) + value.shape)

    def halves(value):
        return [lax.dynamic_slice_in_dim(value, k * half, half, 0) for k in (c_id, 1 - c_id)]

    def whole(mine, other):
        return jnp.where(
            c_id == 0,
            jnp.concatenate([mine, other], axis=-2),
            jnp.concatenate([other, mine], axis=-2),
        )

    def with_transpose(panel, where):
        (parts,) = call(
            scatter_kernel,
            [((steps, nodes_here, classes), BF)],
            [where] + scalars,
            [tiles, panel],
            interpret=interpret,
        )
        parts = lax.all_to_all(parts, "q", 0, 0, tiled=True).astype(F32)
        before = jnp.sum(jnp.where(from_same, 0.0, parts), axis=0).astype(BF)
        moved = lax.ppermute(before, "y", [((i + 1) % ny, i) for i in range(ny)])
        total = jnp.sum(jnp.where(from_same, parts, 0.0), axis=0) + moved.astype(F32)
        mine, away = halves(total)
        pair = (mine + lax.ppermute(away.astype(BF), yrep, pairs).astype(F32)).astype(BF)
        group = lax.all_to_all(
            to_all(pair, nzh), yrep, 0, 0, axis_index_groups=fours, tiled=True
        )
        return ((1.0 - ALPHA) * jnp.sum(group.astype(F32), axis=0)).astype(BF)

    def with_plain(mine, where):
        here = whole(mine, lax.ppermute(mine, yrep, pairs))
        before = lax.ppermute(here, "y", [(i, (i + 1) % ny) for i in range(ny)])
        panels = jnp.where(from_same, here[None], before[None])
        panels = lax.all_to_all(panels, "q", 0, 0, tiled=True)
        mine, away = call(
            gather_kernel,
            [((half, classes), F32), ((half, classes), BF)],
            [where] + scalars,
            [tiles, panels],
            [pltpu.VMEM((nodes_here, classes), F32)],
            interpret=interpret,
        )
        chip = (mine + lax.ppermute(away, "c", cores).astype(F32)).astype(BF)
        chips = lax.all_to_all(to_all(chip, nzh), "zh", 0, 0, tiled=True)
        return (1.0 - ALPHA) * jnp.sum(chips.astype(F32), axis=0)

    hidden = jax.nn.relu(jnp.dot(features, w_first, preferred_element_type=F32)).astype(BF)
    base = jnp.dot(hidden, w_second, preferred_element_type=F32).astype(BF)
    base_half = lax.dynamic_slice_in_dim(base, c_id * half, half, 0)

    current = with_transpose(base, diagonal)
    mixed = with_plain(current, plain) + ALPHA * base_half.astype(F32)
    labels_half = lax.dynamic_slice_in_dim(labels, c_id * half, half, 0)
    onehot = (labels_half[:, None] == jnp.arange(classes, dtype=jnp.int32)[None, :]).astype(F32)
    top = jnp.max(mixed, axis=1, keepdims=True)
    grown = jnp.exp(mixed - top)
    mass = jnp.sum(grown, axis=1, keepdims=True)
    picked = jnp.sum(mixed * onehot, axis=1, keepdims=True)
    ce_sum = jnp.sum(jnp.log(mass) + top - picked)
    grad_out = (grown / mass - onehot) * (1.0 / math.sqrt(nodes))
    both = jnp.stack([grad_out.astype(BF), mixed.astype(BF)])
    both = whole(both, lax.ppermute(both, "c", cores))
    moving, logits = both[0], both[1]

    moving = with_transpose(moving, plain)
    grad_half = (with_plain(moving, diagonal) + ALPHA * grad_out).astype(BF)
    grad_b = whole(grad_half, lax.ppermute(grad_half, "c", cores))

    part = hidden.shape[1] // nc
    bands = part // classes
    hidden_part = lax.dynamic_slice_in_dim(hidden, c_id * part, part, 1)
    second_part = lax.dynamic_slice_in_dim(w_second, c_id * part, part, 0)
    back = lax.dot_general(grad_b, second_part, (((1,), (1,)), ((), ())), preferred_element_type=F32)
    grad_hidden = jnp.where(hidden_part > 0, back, 0.0).astype(BF)
    first = lax.dot_general(
        features, grad_hidden, (((0,), (0,)), ((), ())), preferred_element_type=F32
    ).astype(BF)
    second = lax.dot_general(
        hidden_part, grad_b, (((0,), (0,)), ((), ())), preferred_element_type=F32
    ).astype(BF)
    width = features.shape[1]
    used = bands * width + part
    each = -(-(used + 1) // nblk)
    each = -(-each // 16) * 16
    lanes = lax.broadcasted_iota(jnp.int32, (1, classes), 1)

    def in_terms(value):
        high = value.astype(BF)
        middle = (value - high.astype(F32)).astype(BF)
        low = (value - high.astype(F32) - middle.astype(F32)).astype(BF)
        zero = jnp.zeros((), BF)
        return jnp.where(
            lanes == 0, high, jnp.where(lanes == 1, middle, jnp.where(lanes == 2, low, zero))
        )

    sums = jnp.concatenate(
        [first[:, k * classes : (k + 1) * classes] for k in range(bands)]
        + [second, in_terms(ce_sum), jnp.zeros((each * nblk - used - 1, classes), BF)]
    )
    sums = lax.all_to_all(sums.reshape(nblk, each, classes), BLK, 0, 0, tiled=True)
    sums = jnp.sum(sums.astype(F32), axis=0)
    rows = lax.broadcasted_iota(jnp.int32, (each, classes), 0)
    is_loss = (lax.axis_index(BLK) * each + rows) == used
    loss_sum = jnp.sum(sums[used % each, :3])
    sums = jnp.where(is_loss, in_terms(loss_sum), sums.astype(BF))
    sums = lax.all_to_all(to_all(sums, nblk), BLK, 0, 0, tiled=True).reshape(nblk * each, classes)
    other = lax.ppermute(sums, "c", cores)
    first_core = jnp.where(c_id == 0, sums, other).astype(F32)
    second_core = jnp.where(c_id == 0, other, sums).astype(F32)
    grad_first = jnp.concatenate(
        [v[k * width : (k + 1) * width] for v in (first_core, second_core) for k in range(bands)],
        axis=1,
    )
    grad_second = jnp.concatenate([v[bands * width : used] for v in (first_core, second_core)])
    loss = (jnp.sum(first_core[used, :3]) + jnp.sum(second_core[used, :3])) / nodes
    return (logits, grad_first, grad_second, loss)


def solution(mesh, interpret=False):
    nblk, nrep = mesh.devices.shape
    cores = 2
    fine = Mesh(
        mesh.devices.reshape(nrep, nblk // nrep, nrep // cores, cores), ("y", "q", "zh", "c")
    )
    in_specs = (
        P(BLK, None),
        P(BLK),
        P(),
        P(),
        P(BLK, REP, None, None),
        P(BLK, REP, None, None),
        P(BLK, REP, None, None, None, None),
    )
    out_specs = (P(BLK, None), P(), P(), P())
    return jax.shard_map(
        functools.partial(on_device, interpret),
        mesh=fine,
        in_specs=in_specs,
        out_specs=out_specs,
        check_vma=False,
    )
```

```python
import functools
import math

import jax
import jax.numpy as jnp
from jax import lax
from jax.experimental import pallas as pl
from jax.experimental.pallas import tpu as pltpu
from jax.sharding import Mesh
from jax.sharding import PartitionSpec as P

ALPHA = 0.1
BF = jnp.bfloat16
F32 = jnp.float32
REP = ("zh", "c")
BLK = ("y", "q")


def scatter_kernel(place_ref, rows_ref, cols_ref, tiles_ref, panel_ref, mine_ref, away_ref):
    steps, slots, width, _ = tiles_ref.shape
    q = place_ref[0]
    c = place_ref[1]
    share = jnp.where(place_ref[2] == 1, ALPHA / (1.0 - ALPHA), 0.0).astype(F32)
    for t in range(steps):
        place = lax.rem(q + (steps - t), steps)
        products = []
        for p in range(slots):
            rows = pl.ds(pl.multiple_of(rows_ref[p, t] * width, width), width)
            products.append(
                lax.dot_general(
                    tiles_ref[t, p],
                    panel_ref[rows, :],
                    (((0,), (0,)), ((), ())),
                    preferred_element_type=F32,
                )
            )
        for block, out_ref in ((c, mine_ref), (1 - c, away_ref)):
            total = jnp.zeros(products[0].shape, F32)
            for p in range(slots):
                total = total + jnp.where(cols_ref[p, t] == block, products[p], 0.0)
            if t == 0:
                rows = pl.ds(pl.multiple_of(block * width, width), width)
                total = total + share * panel_ref[rows, :].astype(F32)
            out_ref[place] = total.astype(out_ref.dtype)


def gather_kernel(
    place_ref, rows_ref, cols_ref, tiles_ref, near_ref, far_ref, mine_ref, away_ref, sum_ref
):
    steps, slots, width, _ = tiles_ref.shape
    q = place_ref[0]
    c = place_ref[1]
    share = jnp.where(place_ref[2] == 1, ALPHA / (1.0 - ALPHA), 0.0).astype(F32)
    mine = pl.ds(pl.multiple_of(c * width, width), width)
    away = pl.ds(pl.multiple_of((1 - c) * width, width), width)
    sum_ref[mine, :] = share * near_ref[q].astype(F32)
    sum_ref[away, :] = share * far_ref[q].astype(F32)
    for t in range(steps):
        place = lax.rem(q + (steps - t), steps)
        for p in range(slots):
            piece = jnp.where(cols_ref[p, t] == c, near_ref[place], far_ref[place])
            rows = pl.ds(pl.multiple_of(rows_ref[p, t] * width, width), width)
            sum_ref[rows, :] += jnp.dot(tiles_ref[t, p], piece, preferred_element_type=F32)
    mine_ref[...] = sum_ref[mine, :]
    away_ref[...] = sum_ref[away, :].astype(BF)


def call(kernel, outs, scalars, operands, scratch=(), interpret=False):
    vmem = pl.BlockSpec(memory_space=pltpu.VMEM)
    smem = pl.BlockSpec(memory_space=pltpu.SMEM)
    shapes = [jax.ShapeDtypeStruct(shape, dtype) for shape, dtype in outs]
    return pl.pallas_call(
        kernel,
        out_shape=shapes,
        in_specs=[smem] * len(scalars) + [vmem] * len(operands),
        out_specs=[vmem] * len(outs),
        scratch_shapes=list(scratch),
        compiler_params=pltpu.CompilerParams(vmem_limit_bytes=16 << 20),
        interpret=interpret,
    )(*scalars, *operands)


def on_device(interpret, features, labels, w_first, w_second, block_rows, block_cols, block_vals):
    nodes_here = features.shape[0]
    classes = w_second.shape[1]
    ny, nq, nzh, nc = (lax.axis_size(a) for a in ("y", "q", "zh", "c"))
    nrep = nzh * nc
    nblk = ny * nq
    q_id = lax.axis_index("q")
    c_id = lax.axis_index("c")
    rep_id = lax.axis_index(REP)
    nodes = nodes_here * nblk
    tiles = block_vals[0, 0]
    steps = tiles.shape[0]
    half = nodes_here // nc
    yrep = ("y",) + REP
    fours = [
        [((y + zh * nc + c) % ny) * nrep + zh * nc + c for zh in range(nzh)]
        for y in range(ny)
        for c in range(nc)
    ]
    pairs = []
    for y in range(ny):
        for zh in range(nzh):
            here, there = y * nrep + zh * nc, ((y + 1) % ny) * nrep + zh * nc + 1
            pairs += [(here, there), (there, here)]
    cores = [(0, 1), (1, 0)]
    scalars = [block_rows[0, 0].T, block_cols[0, 0].T]

    def place(flag):
        return jnp.stack([q_id, c_id, flag]).astype(jnp.int32)

    plain = place(jnp.int32(0))
    diagonal = place((rep_id == 0).astype(jnp.int32))
    from_same = (jnp.arange(nq, dtype=jnp.int32) >= q_id)[:, None, None]

    def to_all(value, count):
        return jnp.broadcast_to(value[None], (count,) + value.shape)

    def whole(mine, other):
        return jnp.where(
            c_id == 0,
            jnp.concatenate([mine, other], axis=-2),
            jnp.concatenate([other, mine], axis=-2),
        )

    def with_transpose(panel, where):
        mine, away = call(
            scatter_kernel,
            [((steps, half, classes), F32), ((steps, half, classes), BF)],
            [where] + scalars,
            [tiles, panel],
            interpret=interpret,
        )
        parts = (mine + lax.ppermute(away, yrep, pairs).astype(F32)).astype(BF)
        parts = lax.all_to_all(parts, "q", 0, 0, tiled=True).astype(F32)
        before = jnp.sum(jnp.where(from_same, 0.0, parts), axis=0).astype(BF)
        moved = lax.ppermute(before, "y", [((i + 1) % ny, i) for i in range(ny)])
        total = jnp.sum(jnp.where(from_same, parts, 0.0), axis=0) + moved.astype(F32)
        group = lax.all_to_all(
            to_all(total.astype(BF), nzh), yrep, 0, 0, axis_index_groups=fours, tiled=True
        )
        return ((1.0 - ALPHA) * jnp.sum(group.astype(F32), axis=0)).astype(BF)

    def with_plain(here, where):
        before = lax.ppermute(here, "y", [(i, (i + 1) % ny) for i in range(ny)])
        near = jnp.where(from_same, here[None], before[None])
        near = lax.all_to_all(near, "q", 0, 0, tiled=True)
        far = lax.ppermute(near, yrep, pairs)
        mine, away = call(
            gather_kernel,
            [((half, classes), F32), ((half, classes), BF)],
            [where] + scalars,
            [tiles, near, far],
            [pltpu.VMEM((nodes_here, classes), F32)],
            interpret=interpret,
        )
        chip = (mine + lax.ppermute(away, "c", cores).astype(F32)).astype(BF)
        chips = lax.all_to_all(to_all(chip, nzh), "zh", 0, 0, tiled=True)
        return (1.0 - ALPHA) * jnp.sum(chips.astype(F32), axis=0)

    hidden = jax.nn.relu(jnp.dot(features, w_first, preferred_element_type=F32)).astype(BF)
    base = jnp.dot(hidden, w_second, preferred_element_type=F32).astype(BF)
    base_half = lax.dynamic_slice_in_dim(base, c_id * half, half, 0)

    current = with_transpose(base, diagonal)
    mixed = with_plain(current, plain) + ALPHA * base_half.astype(F32)
    labels_half = lax.dynamic_slice_in_dim(labels, c_id * half, half, 0)
    onehot = (labels_half[:, None] == jnp.arange(classes, dtype=jnp.int32)[None, :]).astype(F32)
    top = jnp.max(mixed, axis=1, keepdims=True)
    grown = jnp.exp(mixed - top)
    mass = jnp.sum(grown, axis=1, keepdims=True)
    picked = jnp.sum(mixed * onehot, axis=1, keepdims=True)
    ce_sum = jnp.sum(jnp.log(mass) + top - picked)
    grad_out = (grown / mass - onehot) * (1.0 / math.sqrt(nodes))
    both = jnp.stack([grad_out.astype(BF), mixed.astype(BF)])
    both = whole(both, lax.ppermute(both, "c", cores))
    moving, logits = both[0], both[1]

    moving = with_transpose(moving, plain)
    grad_half = (with_plain(moving, diagonal) + ALPHA * grad_out).astype(BF)
    grad_b = whole(grad_half, lax.ppermute(grad_half, "c", cores))

    part = hidden.shape[1] // nc
    bands = part // classes
    hidden_part = lax.dynamic_slice_in_dim(hidden, c_id * part, part, 1)
    second_part = lax.dynamic_slice_in_dim(w_second, c_id * part, part, 0)
    back = lax.dot_general(grad_b, second_part, (((1,), (1,)), ((), ())), preferred_element_type=F32)
    grad_hidden = jnp.where(hidden_part > 0, back, 0.0).astype(BF)
    first = lax.dot_general(
        features, grad_hidden, (((0,), (0,)), ((), ())), preferred_element_type=F32
    ).astype(BF)
    second = lax.dot_general(
        hidden_part, grad_b, (((0,), (0,)), ((), ())), preferred_element_type=F32
    ).astype(BF)
    width = features.shape[1]
    used = bands * width + part
    each = -(-(used + 1) // nblk)
    each = -(-each // 16) * 16
    lanes = lax.broadcasted_iota(jnp.int32, (1, classes), 1)

    def in_terms(value):
        high = value.astype(BF)
        middle = (value - high.astype(F32)).astype(BF)
        low = (value - high.astype(F32) - middle.astype(F32)).astype(BF)
        zero = jnp.zeros((), BF)
        return jnp.where(
            lanes == 0, high, jnp.where(lanes == 1, middle, jnp.where(lanes == 2, low, zero))
        )

    sums = jnp.concatenate(
        [first[:, k * classes : (k + 1) * classes] for k in range(bands)]
        + [second, in_terms(ce_sum), jnp.zeros((each * nblk - used - 1, classes), BF)]
    )
    sums = lax.all_to_all(sums.reshape(nblk, each, classes), BLK, 0, 0, tiled=True)
    sums = jnp.sum(sums.astype(F32), axis=0)
    rows = lax.broadcasted_iota(jnp.int32, (each, classes), 0)
    is_loss = (lax.axis_index(BLK) * each + rows) == used
    loss_sum = jnp.sum(sums[used % each, :3])
    sums = jnp.where(is_loss, in_terms(loss_sum), sums.astype(BF))
    sums = lax.all_to_all(to_all(sums, nblk), BLK, 0, 0, tiled=True).reshape(nblk * each, classes)
    other = lax.ppermute(sums, "c", cores)
    first_core = jnp.where(c_id == 0, sums, other).astype(F32)
    second_core = jnp.where(c_id == 0, other, sums).astype(F32)
    grad_first = jnp.concatenate(
        [v[k * width : (k + 1) * width] for v in (first_core, second_core) for k in range(bands)],
        axis=1,
    )
    grad_second = jnp.concatenate([v[bands * width : used] for v in (first_core, second_core)])
    loss = (jnp.sum(first_core[used, :3]) + jnp.sum(second_core[used, :3])) / nodes
    return (logits, grad_first, grad_second, loss)


def solution(mesh, interpret=False):
    nblk, nrep = mesh.devices.shape
    cores = 2
    fine = Mesh(
        mesh.devices.reshape(nrep, nblk // nrep, nrep // cores, cores), ("y", "q", "zh", "c")
    )
    in_specs = (
        P(BLK, None),
        P(BLK),
        P(),
        P(),
        P(BLK, REP, None, None),
        P(BLK, REP, None, None),
        P(BLK, REP, None, None, None, None),
    )
    out_specs = (P(BLK, None), P(), P(), P())
    return jax.shard_map(
        functools.partial(on_device, interpret),
        mesh=fine,
        in_specs=in_specs,
        out_specs=out_specs,
        check_vma=False,
    )
```

```python
import functools
import math

import jax
import jax.numpy as jnp
from jax import lax
from jax.experimental import pallas as pl
from jax.experimental.pallas import tpu as pltpu
from jax.sharding import Mesh
from jax.sharding import PartitionSpec as P

ALPHA = 0.1
BF = jnp.bfloat16
F32 = jnp.float32
REP = ("zh", "c")
BLK = ("y", "q")


def scatter_kernel(
    place_ref, rows_ref, cols_ref, far_tiles_ref, panel_ref, mine_ref, away_ref, tiles_ref, arrived
):
    steps, slots, width, _ = tiles_ref.shape
    q = place_ref[0]
    c = place_ref[1]
    share = jnp.where(place_ref[2] == 1, ALPHA / (1.0 - ALPHA), 0.0).astype(F32)
    copies = [
        pltpu.make_async_copy(far_tiles_ref.at[t], tiles_ref.at[t], arrived.at[t])
        for t in range(steps)
    ]
    for copy in copies:
        copy.start()
    for t in range(steps):
        copies[t].wait()
        place = lax.rem(q + (steps - t), steps)
        products = []
        for p in range(slots):
            rows = pl.ds(pl.multiple_of(rows_ref[p, t] * width, width), width)
            products.append(
                lax.dot_general(
                    tiles_ref[t, p],
                    panel_ref[rows, :],
                    (((0,), (0,)), ((), ())),
                    preferred_element_type=F32,
                )
            )
        for block, out_ref in ((c, mine_ref), (1 - c, away_ref)):
            total = jnp.zeros(products[0].shape, F32)
            for p in range(slots):
                total = total + jnp.where(cols_ref[p, t] == block, products[p], 0.0)
            if t == 0:
                rows = pl.ds(pl.multiple_of(block * width, width), width)
                total = total + share * panel_ref[rows, :].astype(F32)
            out_ref[place] = total.astype(out_ref.dtype)


def gather_kernel(
    place_ref, rows_ref, cols_ref, tiles_ref, near_ref, far_ref, mine_ref, away_ref, sum_ref
):
    steps, slots, width, _ = tiles_ref.shape
    q = place_ref[0]
    c = place_ref[1]
    share = jnp.where(place_ref[2] == 1, ALPHA / (1.0 - ALPHA), 0.0).astype(F32)
    mine = pl.ds(pl.multiple_of(c * width, width), width)
    away = pl.ds(pl.multiple_of((1 - c) * width, width), width)
    sum_ref[mine, :] = share * near_ref[q].astype(F32)
    sum_ref[away, :] = share * far_ref[q].astype(F32)
    for t in range(steps):
        place = lax.rem(q + (steps - t), steps)
        for p in range(slots):
            piece = jnp.where(cols_ref[p, t] == c, near_ref[place], far_ref[place])
            rows = pl.ds(pl.multiple_of(rows_ref[p, t] * width, width), width)
            sum_ref[rows, :] += jnp.dot(tiles_ref[t, p], piece, preferred_element_type=F32)
    mine_ref[...] = sum_ref[mine, :]
    away_ref[...] = sum_ref[away, :].astype(BF)


def call(kernel, outs, scalars, tiles, operands, scratch, tiles_space, interpret):
    vmem = pl.BlockSpec(memory_space=pltpu.VMEM)
    smem = pl.BlockSpec(memory_space=pltpu.SMEM)
    shapes = [jax.ShapeDtypeStruct(shape, dtype) for shape, dtype in outs]
    return pl.pallas_call(
        kernel,
        out_shape=shapes,
        in_specs=[smem] * len(scalars)
        + [pl.BlockSpec(memory_space=tiles_space)]
        + [vmem] * len(operands),
        out_specs=[vmem] * len(outs),
        scratch_shapes=list(scratch),
        compiler_params=pltpu.CompilerParams(vmem_limit_bytes=16 << 20),
        interpret=interpret,
    )(*scalars, tiles, *operands)


def on_device(interpret, features, labels, w_first, w_second, block_rows, block_cols, block_vals):
    nodes_here = features.shape[0]
    classes = w_second.shape[1]
    ny, nq, nzh, nc = (lax.axis_size(a) for a in ("y", "q", "zh", "c"))
    nrep = nzh * nc
    nblk = ny * nq
    q_id = lax.axis_index("q")
    c_id = lax.axis_index("c")
    rep_id = lax.axis_index(REP)
    nodes = nodes_here * nblk
    tiles = block_vals[0, 0]
    far_tiles = pltpu.with_memory_space_constraint(tiles, pltpu.HBM)
    steps = tiles.shape[0]
    half = nodes_here // nc
    yrep = ("y",) + REP
    fours = [
        [((y + zh * nc + c) % ny) * nrep + zh * nc + c for zh in range(nzh)]
        for y in range(ny)
        for c in range(nc)
    ]
    pairs = []
    for y in range(ny):
        for zh in range(nzh):
            here, there = y * nrep + zh * nc, ((y + 1) % ny) * nrep + zh * nc + 1
            pairs += [(here, there), (there, here)]
    cores = [(0, 1), (1, 0)]
    scalars = [block_rows[0, 0].T, block_cols[0, 0].T]

    def place(flag):
        return jnp.stack([q_id, c_id, flag]).astype(jnp.int32)

    width = features.shape[1]
    part = w_first.shape[1] // nc
    bands = part // classes
    used = bands * width + part
    each = -(-(used + 3) // nq)
    each = -(-each // 16) * 16
    plain = place(jnp.int32(0))
    diagonal = place((rep_id == 0).astype(jnp.int32))
    from_same = lax.broadcasted_iota(jnp.int32, (nq, 1, classes), 0) >= q_id
    loss_row = lax.broadcasted_iota(jnp.int32, (each, classes), 0) - (used - q_id * each)
    labels_half = lax.dynamic_slice_in_dim(labels, c_id * half, half, 0)

    def in_terms(value):
        high = value.astype(BF)
        middle = (value - high.astype(F32)).astype(BF)
        low = (value - high.astype(F32) - middle.astype(F32)).astype(BF)
        return high, middle, low

    def summed(parts):
        sums = jnp.sum(parts.astype(F32), axis=0)
        at = used % each
        terms = in_terms(jnp.sum(sums[at : at + 3], axis=0, keepdims=True))
        sums = sums.astype(BF)
        for k, term in enumerate(terms):
            sums = jnp.where(loss_row == k, term, sums)
        return sums


    def to_all(value, count):
        return jnp.broadcast_to(value[None], (count,) + value.shape)

    def whole(mine, other):
        return jnp.where(
            c_id == 0,
            jnp.concatenate([mine, other], axis=-2),
            jnp.concatenate([other, mine], axis=-2),
        )

    def with_transpose(panel, where):
        mine, away = call(
            scatter_kernel,
            [((steps, half, classes), F32), ((steps, half, classes), BF)],
            [where] + scalars,
            far_tiles,
            [panel],
            [pltpu.VMEM(tiles.shape, BF), pltpu.SemaphoreType.DMA((steps,))],
            pltpu.HBM,
            interpret,
        )
        parts = (mine + lax.ppermute(away, yrep, pairs).astype(F32)).astype(BF)
        parts = lax.all_to_all(parts, "q", 0, 0, tiled=True).astype(F32)
        before = jnp.sum(jnp.where(from_same, 0.0, parts), axis=0).astype(BF)
        moved = lax.ppermute(before, "y", [((i + 1) % ny, i) for i in range(ny)])
        total = jnp.sum(jnp.where(from_same, parts, 0.0), axis=0) + moved.astype(F32)
        group = lax.all_to_all(
            to_all(total.astype(BF), nzh), yrep, 0, 0, axis_index_groups=fours, tiled=True
        )
        return ((1.0 - ALPHA) * jnp.sum(group.astype(F32), axis=0)).astype(BF)

    def with_plain(here, where):
        before = lax.ppermute(here, "y", [(i, (i + 1) % ny) for i in range(ny)])
        near = jnp.where(from_same, here[None], before[None])
        near = lax.all_to_all(near, "q", 0, 0, tiled=True)
        far = lax.ppermute(near, yrep, pairs)
        mine, away = call(
            gather_kernel,
            [((half, classes), F32), ((half, classes), BF)],
            [where] + scalars,
            tiles,
            [near, far],
            [pltpu.VMEM((nodes_here, classes), F32)],
            pltpu.VMEM,
            interpret,
        )
        chip = (mine + lax.ppermute(away, "c", cores).astype(F32)).astype(BF)
        chips = lax.all_to_all(to_all(chip, nzh), "zh", 0, 0, tiled=True)
        return (1.0 - ALPHA) * jnp.sum(chips.astype(F32), axis=0)

    hidden = jax.nn.relu(jnp.dot(features, w_first, preferred_element_type=F32)).astype(BF)
    base = jnp.dot(hidden, w_second, preferred_element_type=F32).astype(BF)
    base_half = lax.dynamic_slice_in_dim(base, c_id * half, half, 0)
    base, base_half, labels_half, plain, diagonal, from_same, loss_row = lax.optimization_barrier(
        (base, base_half, labels_half, plain, diagonal, from_same, loss_row)
    )

    current = with_transpose(base, diagonal)
    mixed = with_plain(current, plain) + ALPHA * base_half.astype(F32)
    onehot = (labels_half[:, None] == jnp.arange(classes, dtype=jnp.int32)[None, :]).astype(F32)
    top = jnp.max(mixed, axis=1, keepdims=True)
    grown = jnp.exp(mixed - top)
    mass = jnp.sum(grown, axis=1, keepdims=True)
    lanes = lax.broadcasted_iota(jnp.int32, (1, classes), 1)
    ce_rows = jnp.where(lanes == 0, jnp.log(mass) + top, 0.0) - mixed * onehot
    ce_terms = in_terms(jnp.sum(ce_rows, axis=0, keepdims=True))
    grad_out = (grown / mass - onehot) * (1.0 / math.sqrt(nodes))
    both, ce_terms, grad_out = lax.optimization_barrier(
        (jnp.stack([grad_out.astype(BF), mixed.astype(BF)]), ce_terms, grad_out)
    )
    both = whole(both, lax.ppermute(both, "c", cores))
    moving, logits = both[0], both[1]

    moving = with_transpose(moving, plain)
    grad_half = (with_plain(moving, diagonal) + ALPHA * grad_out).astype(BF)
    grad_b = whole(grad_half, lax.ppermute(grad_half, "c", cores))

    hidden_part = lax.dynamic_slice_in_dim(hidden, c_id * part, part, 1)
    second_part = lax.dynamic_slice_in_dim(w_second, c_id * part, part, 0)
    back = lax.dot_general(grad_b, second_part, (((1,), (1,)), ((), ())), preferred_element_type=F32)
    grad_hidden = jnp.where(hidden_part > 0, back, 0.0).astype(BF)
    first = lax.dot_general(
        features, grad_hidden, (((0,), (0,)), ((), ())), preferred_element_type=F32
    ).astype(BF)
    second = lax.dot_general(
        hidden_part, grad_b, (((0,), (0,)), ((), ())), preferred_element_type=F32
    ).astype(BF)

    sums = jnp.concatenate(
        [first[:, k * classes : (k + 1) * classes] for k in range(bands)]
        + [second, *ce_terms, jnp.zeros((each * nq - used - 3, classes), BF)]
    ).reshape(nq, each, classes)
    sums = summed(lax.all_to_all(sums, "q", 0, 0, tiled=True))
    sums = summed(lax.all_to_all(to_all(sums, ny), "y", 0, 0, tiled=True))
    sums = lax.all_to_all(to_all(sums, nq), "q", 0, 0, tiled=True).reshape(nq * each, classes)
    other = lax.ppermute(sums, "c", cores)
    first_core = jnp.where(c_id == 0, sums, other).astype(F32)
    second_core = jnp.where(c_id == 0, other, sums).astype(F32)
    grad_first = jnp.concatenate(
        [v[k * width : (k + 1) * width] for v in (first_core, second_core) for k in range(bands)],
        axis=1,
    )
    grad_second = jnp.concatenate([v[bands * width : used] for v in (first_core, second_core)])
    loss = jnp.sum(first_core[used : used + 3] + second_core[used : used + 3]) / nodes
    return (logits, grad_first, grad_second, loss)


def solution(mesh, interpret=False):
    nblk, nrep = mesh.devices.shape
    cores = 2
    fine = Mesh(
        mesh.devices.reshape(nrep, nblk // nrep, nrep // cores, cores), ("y", "q", "zh", "c")
    )
    in_specs = (
        P(BLK, None),
        P(BLK),
        P(),
        P(),
        P(BLK, REP, None, None),
        P(BLK, REP, None, None),
        P(BLK, REP, None, None, None, None),
    )
    out_specs = (P(BLK, None), P(), P(), P())
    return jax.shard_map(
        functools.partial(on_device, interpret),
        mesh=fine,
        in_specs=in_specs,
        out_specs=out_specs,
        check_vma=False,
    )
```

```python
import functools
import math

import jax
import jax.numpy as jnp
from jax import lax
from jax.experimental import pallas as pl
from jax.experimental.pallas import tpu as pltpu
from jax.sharding import Mesh
from jax.sharding import PartitionSpec as P

ALPHA = 0.1
BF = jnp.bfloat16
F32 = jnp.float32
REP = ("zh", "c")
BLK = ("y", "q")


def share_of(flag):
    return jnp.where(flag == 1, ALPHA / (1.0 - ALPHA), 0.0).astype(F32)


def scatter_kernel(place_ref, rows_ref, cols_ref, tiles_ref, panel_ref, mine_ref, away_ref):
    steps, slots, width, _ = tiles_ref.shape
    q = place_ref[0]
    c = place_ref[1]
    share = share_of(place_ref[2])
    for t in range(steps):
        place = lax.rem(q + (steps - t), steps)
        products = []
        for p in range(slots):
            rows = pl.ds(pl.multiple_of(rows_ref[p, t] * width, width), width)
            products.append(
                lax.dot_general(
                    tiles_ref[t, p],
                    panel_ref[rows, :],
                    (((0,), (0,)), ((), ())),
                    preferred_element_type=F32,
                )
            )
        for block, out_ref in ((c, mine_ref), (1 - c, away_ref)):
            total = jnp.zeros(products[0].shape, F32)
            for p in range(slots):
                total = total + jnp.where(cols_ref[p, t] == block, products[p], 0.0)
            if t == 0:
                rows = pl.ds(pl.multiple_of(block * width, width), width)
                total = total + share * panel_ref[rows, :].astype(F32)
            out_ref[place] = total.astype(out_ref.dtype)


def first_kernel(
    place_ref,
    rows_ref,
    cols_ref,
    far_tiles_ref,
    far_features_ref,
    far_first_ref,
    far_second_ref,
    mine_ref,
    away_ref,
    tiles_ref,
    hidden_ref,
    base_ref,
    features_ref,
    first_ref,
    second_ref,
    arrived,
):
    copies = [
        pltpu.make_async_copy(source, target, arrived.at[k])
        for k, (source, target) in enumerate(
            (
                (far_features_ref, features_ref),
                (far_first_ref, first_ref),
                (far_second_ref, second_ref),
                (far_tiles_ref, tiles_ref),
            )
        )
    ]
    for copy in copies:
        copy.start()
    copies[0].wait()
    copies[1].wait()
    hidden = jnp.dot(features_ref[...], first_ref[...], preferred_element_type=F32)
    hidden_ref[...] = jnp.maximum(hidden, 0.0).astype(BF)
    copies[2].wait()
    base = jnp.dot(hidden_ref[...], second_ref[...], preferred_element_type=F32)
    base_ref[...] = base.astype(BF)
    copies[3].wait()
    scatter_kernel(place_ref, rows_ref, cols_ref, tiles_ref, base_ref, mine_ref, away_ref)


def add_gathered(place_ref, rows_ref, cols_ref, tiles_ref, near_ref, far_ref, sum_ref):
    steps, slots, width, _ = tiles_ref.shape
    q = place_ref[0]
    c = place_ref[1]
    for t in range(steps):
        place = lax.rem(q + (steps - t), steps)
        for p in range(slots):
            piece = jnp.where(cols_ref[p, t] == c, near_ref[place], far_ref[place])
            rows = pl.ds(pl.multiple_of(rows_ref[p, t] * width, width), width)
            sum_ref[rows, :] += jnp.dot(tiles_ref[t, p], piece, preferred_element_type=F32)


def core_rows(place_ref, width):
    c = place_ref[1]
    return [pl.ds(pl.multiple_of(k * width, width), width) for k in (c, 1 - c)]


def gather_kernel(
    place_ref, rows_ref, cols_ref, tiles_ref, near_ref, far_ref, mine_ref, away_ref, sum_ref
):
    mine, away = core_rows(place_ref, tiles_ref.shape[2])
    sum_ref[...] = jnp.zeros(sum_ref.shape, F32)
    add_gathered(place_ref, rows_ref, cols_ref, tiles_ref, near_ref, far_ref, sum_ref)
    mine_ref[...] = sum_ref[mine, :]
    away_ref[...] = sum_ref[away, :].astype(BF)


def last_kernel(
    place_ref, rows_ref, cols_ref, tiles_ref, near_ref, far_ref, grad_ref, out_ref, sum_ref
):
    mine, away = core_rows(place_ref, tiles_ref.shape[2])
    q = place_ref[0]
    share = share_of(place_ref[2])
    sum_ref[mine, :] = share * (near_ref[q].astype(F32) + grad_ref[mine, :].astype(F32))
    sum_ref[away, :] = share * (far_ref[q].astype(F32) + grad_ref[away, :].astype(F32))
    add_gathered(place_ref, rows_ref, cols_ref, tiles_ref, near_ref, far_ref, sum_ref)
    out_ref[...] = ((1.0 - ALPHA) * sum_ref[...]).astype(BF)


def call(kernel, outs, scalars, operands, scratch=(), space=pltpu.VMEM, interpret=False):
    vmem = pl.BlockSpec(memory_space=pltpu.VMEM)
    smem = pl.BlockSpec(memory_space=pltpu.SMEM)
    shapes = [jax.ShapeDtypeStruct(shape, dtype) for shape, dtype in outs]
    if not interpret:
        operands = [pltpu.with_memory_space_constraint(v, space) for v in operands]
    return pl.pallas_call(
        kernel,
        out_shape=shapes,
        in_specs=[smem] * len(scalars) + [pl.BlockSpec(memory_space=space)] * len(operands),
        out_specs=[vmem] * len(outs),
        scratch_shapes=list(scratch),
        compiler_params=pltpu.CompilerParams(vmem_limit_bytes=16 << 20),
        interpret=interpret,
    )(*scalars, *operands)


def on_device(interpret, features, labels, w_first, w_second, block_rows, block_cols, block_vals):
    nodes_here = features.shape[0]
    classes = w_second.shape[1]
    ny, nq, nzh, nc = (lax.axis_size(a) for a in ("y", "q", "zh", "c"))
    nrep = nzh * nc
    nblk = ny * nq
    q_id = lax.axis_index("q")
    c_id = lax.axis_index("c")
    rep_id = lax.axis_index(REP)
    nodes = nodes_here * nblk
    tiles = block_vals[0, 0]
    steps = tiles.shape[0]
    half = nodes_here // nc
    yrep = ("y",) + REP
    fours = [
        [((y + zh * nc + c) % ny) * nrep + zh * nc + c for zh in range(nzh)]
        for y in range(ny)
        for c in range(nc)
    ]
    pairs = []
    for y in range(ny):
        for zh in range(nzh):
            here, there = y * nrep + zh * nc, ((y + 1) % ny) * nrep + zh * nc + 1
            pairs += [(here, there), (there, here)]
    cores = [(0, 1), (1, 0)]
    scalars = [block_rows[0, 0].T, block_cols[0, 0].T]

    def place(flag):
        return jnp.stack([q_id, c_id, flag]).astype(jnp.int32)

    width = features.shape[1]
    part = w_first.shape[1] // nc
    bands = part // classes
    used = bands * width + part
    each = -(-(used + 3) // nq)
    each = -(-each // 16) * 16
    plain = place(jnp.int32(0))
    diagonal = place((rep_id == 0).astype(jnp.int32))
    from_same = lax.broadcasted_iota(jnp.int32, (nq, 1, classes), 0) >= q_id
    loss_row = lax.broadcasted_iota(jnp.int32, (each, classes), 0) - (used - q_id * each)
    labels_half = lax.dynamic_slice_in_dim(labels, c_id * half, half, 0)

    def in_terms(value):
        high = value.astype(BF)
        middle = (value - high.astype(F32)).astype(BF)
        low = (value - high.astype(F32) - middle.astype(F32)).astype(BF)
        return high, middle, low

    def summed(parts):
        sums = jnp.sum(parts.astype(F32), axis=0)
        at = used % each
        terms = in_terms(jnp.sum(sums[at : at + 3], axis=0, keepdims=True))
        sums = sums.astype(BF)
        for k, term in enumerate(terms):
            sums = jnp.where(loss_row == k, term, sums)
        return sums


    def to_all(value, count):
        return jnp.broadcast_to(value[None], (count,) + value.shape)

    def whole(mine, other):
        return jnp.where(
            c_id == 0,
            jnp.concatenate([mine, other], axis=-2),
            jnp.concatenate([other, mine], axis=-2),
        )

    def reduced(mine, away):
        parts = (mine + lax.ppermute(away, yrep, pairs).astype(F32)).astype(BF)
        parts = lax.all_to_all(parts, "q", 0, 0, tiled=True).astype(F32)
        before = jnp.sum(jnp.where(from_same, 0.0, parts), axis=0).astype(BF)
        moved = lax.ppermute(before, "y", [((i + 1) % ny, i) for i in range(ny)])
        total = jnp.sum(jnp.where(from_same, parts, 0.0), axis=0) + moved.astype(F32)
        group = lax.all_to_all(
            to_all(total.astype(BF), nzh), yrep, 0, 0, axis_index_groups=fours, tiled=True
        )
        return ((1.0 - ALPHA) * jnp.sum(group.astype(F32), axis=0)).astype(BF)

    def gathered(here):
        before = lax.ppermute(here, "y", [(i, (i + 1) % ny) for i in range(ny)])
        near = jnp.where(from_same, here[None], before[None])
        near = lax.all_to_all(near, "q", 0, 0, tiled=True)
        return near, lax.ppermute(near, yrep, pairs)

    slots_here = [((steps, half, classes), F32), ((steps, half, classes), BF)]
    sum_here = pltpu.VMEM((nodes_here, classes), F32)
    labels_half, plain, diagonal, from_same, loss_row = lax.optimization_barrier(
        (labels_half, plain, diagonal, from_same, loss_row)
    )
    operands = (tiles, features, w_first, w_second)
    mine, away, tiles, hidden, base = call(
        first_kernel,
        slots_here
        + [(tiles.shape, BF), ((nodes_here, w_first.shape[1]), BF), ((nodes_here, classes), BF)],
        [diagonal] + scalars,
        operands,
        [pltpu.VMEM(v.shape, BF) for v in operands[1:]] + [pltpu.SemaphoreType.DMA((4,))],
        pltpu.HBM,
        interpret=interpret,
    )
    base_half = lax.dynamic_slice_in_dim(base, c_id * half, half, 0)
    near, far = gathered(reduced(mine, away))
    mine, away = call(
        gather_kernel,
        [((half, classes), F32), ((half, classes), BF)],
        [plain] + scalars,
        [tiles, near, far],
        [sum_here],
        interpret=interpret,
    )
    chip = (mine + lax.ppermute(away, "c", cores).astype(F32)).astype(BF)
    chips = lax.all_to_all(to_all(chip, nzh), "zh", 0, 0, tiled=True)
    mixed = (1.0 - ALPHA) * jnp.sum(chips.astype(F32), axis=0) + ALPHA * base_half.astype(F32)
    chosen = labels_half[:, None] == jnp.arange(classes, dtype=jnp.int32)[None, :]
    top = jnp.max(mixed, axis=1, keepdims=True)
    grown = jnp.exp(mixed - top)
    mass = jnp.sum(grown, axis=1, keepdims=True)
    ce_rows = jnp.where(chosen, jnp.log(mass) + top - mixed, 0.0)
    ce_sum = jnp.sum(ce_rows, axis=0, keepdims=True)
    ce_terms = in_terms(jnp.where(lax.axis_index("zh") == 0, ce_sum, 0.0))
    grad_out = (grown / mass - chosen.astype(F32)) * (1.0 / math.sqrt(nodes))
    both, ce_terms = lax.optimization_barrier(
        (jnp.stack([grad_out.astype(BF), mixed.astype(BF)]), ce_terms)
    )
    both = whole(both, lax.ppermute(both, "c", cores))
    moving, logits = both[0], both[1]

    mine, away = call(
        scatter_kernel, slots_here, [plain] + scalars, [tiles, moving], interpret=interpret
    )
    near, far = gathered(reduced(mine, away))
    (grad_b,) = call(
        last_kernel,
        [((nodes_here, classes), BF)],
        [diagonal] + scalars,
        [tiles, near, far, moving],
        [sum_here],
        interpret=interpret,
    )

    def weight_rows(core):
        hidden_part = lax.dynamic_slice_in_dim(hidden, core * part, part, 1)
        second_part = lax.dynamic_slice_in_dim(w_second, core * part, part, 0)
        back = lax.dot_general(
            grad_b, second_part, (((1,), (1,)), ((), ())), preferred_element_type=F32
        )
        grad_hidden = jnp.where(hidden_part > 0, back, 0.0).astype(BF)
        first = lax.dot_general(
            features, grad_hidden, (((0,), (0,)), ((), ())), preferred_element_type=F32
        )
        second = lax.dot_general(
            hidden_part, grad_b, (((0,), (0,)), ((), ())), preferred_element_type=F32
        )
        bands_here = [first[:, k * classes : (k + 1) * classes] for k in range(bands)]
        return jnp.concatenate(bands_here + [second])

    away = lax.ppermute(weight_rows(1 - c_id).astype(BF), "c", cores)
    sums = (weight_rows(c_id) + away.astype(F32)).astype(BF)
    sums = jnp.concatenate(
        [sums, *ce_terms, jnp.zeros((each * nq - used - 3, classes), BF)]
    ).reshape(nq, each, classes)
    sums = summed(lax.all_to_all(sums, "q", 0, 0, tiled=True))
    sums = summed(lax.all_to_all(to_all(sums, nzh), "zh", 0, 0, tiled=True))
    sums = summed(lax.all_to_all(to_all(sums, ny), "y", 0, 0, tiled=True))
    sums = lax.all_to_all(to_all(sums, nq), "q", 0, 0, tiled=True).reshape(nq * each, classes)
    other = lax.ppermute(sums, "c", cores)
    first_core = jnp.where(c_id == 0, sums, other).astype(F32)
    second_core = jnp.where(c_id == 0, other, sums).astype(F32)
    grad_first = jnp.concatenate(
        [v[k * width : (k + 1) * width] for v in (first_core, second_core) for k in range(bands)],
        axis=1,
    )
    grad_second = jnp.concatenate([v[bands * width : used] for v in (first_core, second_core)])
    loss = jnp.sum(first_core[used : used + 3] + second_core[used : used + 3]) / nodes
    return (logits, grad_first, grad_second, loss)


def solution(mesh, interpret=False):
    nblk, nrep = mesh.devices.shape
    cores = 2
    fine = Mesh(
        mesh.devices.reshape(nrep, nblk // nrep, nrep // cores, cores), ("y", "q", "zh", "c")
    )
    in_specs = (
        P(BLK, None),
        P(BLK),
        P(),
        P(),
        P(BLK, REP, None, None),
        P(BLK, REP, None, None),
        P(BLK, REP, None, None, None, None),
    )
    out_specs = (P(BLK, None), P(), P(), P())
    return jax.shard_map(
        functools.partial(on_device, interpret),
        mesh=fine,
        in_specs=in_specs,
        out_specs=out_specs,
        check_vma=False,
    )
```

```python
import functools
import math

import jax
import jax.numpy as jnp
from jax import lax
from jax.experimental import pallas as pl
from jax.experimental.pallas import tpu as pltpu
from jax.sharding import Mesh
from jax.sharding import PartitionSpec as P

ALPHA = 0.1
BF = jnp.bfloat16
F32 = jnp.float32
REP = ("zh", "c")
BLK = ("y", "q")


def share_of(flag):
    return jnp.where(flag == 1, ALPHA / (1.0 - ALPHA), 0.0).astype(F32)


def scatter_kernel(place_ref, rows_ref, cols_ref, tiles_ref, panel_ref, mine_ref, away_ref):
    steps, slots, width, _ = tiles_ref.shape
    q = place_ref[0]
    c = place_ref[1]
    share = share_of(place_ref[2])
    for t in range(steps):
        place = lax.rem(q + (steps - t), steps)
        products = []
        for p in range(slots):
            rows = pl.ds(pl.multiple_of(rows_ref[p, t] * width, width), width)
            products.append(
                lax.dot_general(
                    tiles_ref[t, p],
                    panel_ref[rows, :],
                    (((0,), (0,)), ((), ())),
                    preferred_element_type=F32,
                )
            )
        for block, out_ref in ((c, mine_ref), (1 - c, away_ref)):
            total = jnp.zeros(products[0].shape, F32)
            for p in range(slots):
                total = total + jnp.where(cols_ref[p, t] == block, products[p], 0.0)
            if t == 0:
                rows = pl.ds(pl.multiple_of(block * width, width), width)
                total = total + share * panel_ref[rows, :].astype(F32)
            out_ref[place] = total.astype(out_ref.dtype)


def first_kernel(
    place_ref,
    far_rows_ref,
    far_cols_ref,
    far_tiles_ref,
    far_features_ref,
    far_first_ref,
    far_second_ref,
    mine_ref,
    away_ref,
    tiles_ref,
    far_hidden_ref,
    base_ref,
    features_ref,
    first_ref,
    second_ref,
    hidden_ref,
    rows_ref,
    cols_ref,
    arrived,
):
    copies = [
        pltpu.make_async_copy(source, target, arrived.at[k])
        for k, (source, target) in enumerate(
            (
                (far_features_ref, features_ref),
                (far_first_ref, first_ref),
                (far_second_ref, second_ref),
                (far_tiles_ref, tiles_ref),
                (far_rows_ref, rows_ref),
                (far_cols_ref, cols_ref),
                (hidden_ref, far_hidden_ref),
            )
        )
    ]
    for copy in copies[:6]:
        copy.start()
    copies[0].wait()
    copies[1].wait()
    hidden = jnp.dot(features_ref[...], first_ref[...], preferred_element_type=F32)
    hidden_ref[...] = jnp.maximum(hidden, 0.0).astype(BF)
    copies[6].start()
    copies[2].wait()
    base = jnp.dot(hidden_ref[...], second_ref[...], preferred_element_type=F32)
    base_ref[...] = base.astype(BF)
    for copy in copies[3:6]:
        copy.wait()
    scatter_kernel(place_ref, rows_ref, cols_ref, tiles_ref, base_ref, mine_ref, away_ref)
    copies[6].wait()


def add_gathered(place_ref, rows_ref, cols_ref, tiles_ref, near_ref, far_ref, sum_ref):
    steps, slots, width, _ = tiles_ref.shape
    q = place_ref[0]
    c = place_ref[1]
    for t in range(steps):
        place = lax.rem(q + (steps - t), steps)
        for p in range(slots):
            piece = jnp.where(cols_ref[p, t] == c, near_ref[place], far_ref[place])
            rows = pl.ds(pl.multiple_of(rows_ref[p, t] * width, width), width)
            sum_ref[rows, :] += jnp.dot(tiles_ref[t, p], piece, preferred_element_type=F32)


def core_rows(place_ref, width):
    c = place_ref[1]
    return [pl.ds(pl.multiple_of(k * width, width), width) for k in (c, 1 - c)]


def gather_kernel(
    place_ref, rows_ref, cols_ref, tiles_ref, near_ref, far_ref, mine_ref, away_ref, sum_ref
):
    mine, away = core_rows(place_ref, tiles_ref.shape[2])
    sum_ref[...] = jnp.zeros(sum_ref.shape, F32)
    add_gathered(place_ref, rows_ref, cols_ref, tiles_ref, near_ref, far_ref, sum_ref)
    mine_ref[...] = sum_ref[mine, :]
    away_ref[...] = sum_ref[away, :].astype(BF)


def last_kernel(
    place_ref, rows_ref, cols_ref, tiles_ref, near_ref, far_ref, grad_ref, out_ref, sum_ref
):
    mine, away = core_rows(place_ref, tiles_ref.shape[2])
    q = place_ref[0]
    share = share_of(place_ref[2])
    sum_ref[mine, :] = share * (near_ref[q].astype(F32) + grad_ref[mine, :].astype(F32))
    sum_ref[away, :] = share * (far_ref[q].astype(F32) + grad_ref[away, :].astype(F32))
    add_gathered(place_ref, rows_ref, cols_ref, tiles_ref, near_ref, far_ref, sum_ref)
    out_ref[...] = ((1.0 - ALPHA) * sum_ref[...]).astype(BF)


def call(kernel, outs, scalars, operands, scratch=(), far=(), far_outs=(), interpret=False):
    vmem = pl.BlockSpec(memory_space=pltpu.VMEM)
    smem = pl.BlockSpec(memory_space=pltpu.SMEM)
    hbm = pl.BlockSpec(memory_space=pltpu.HBM)
    far = [v if interpret else pltpu.with_memory_space_constraint(v, pltpu.HBM) for v in far]
    shapes = [
        pltpu.HBM(shape, dtype) if k in far_outs else jax.ShapeDtypeStruct(shape, dtype)
        for k, (shape, dtype) in enumerate(outs)
    ]
    return pl.pallas_call(
        kernel,
        out_shape=shapes,
        in_specs=[smem] * len(scalars) + [hbm] * len(far) + [vmem] * len(operands),
        out_specs=[hbm if k in far_outs else vmem for k in range(len(outs))],
        scratch_shapes=list(scratch),
        compiler_params=pltpu.CompilerParams(vmem_limit_bytes=16 << 20),
        interpret=interpret,
    )(*scalars, *far, *operands)


def on_device(interpret, features, labels, w_first, w_second, block_rows, block_cols, block_vals):
    nodes_here = features.shape[0]
    classes = w_second.shape[1]
    ny, nq, nzh, nc = (lax.axis_size(a) for a in ("y", "q", "zh", "c"))
    nrep = nzh * nc
    nblk = ny * nq
    q_id = lax.axis_index("q")
    c_id = lax.axis_index("c")
    rep_id = lax.axis_index(REP)
    nodes = nodes_here * nblk
    tiles = block_vals[0, 0]
    steps = tiles.shape[0]
    half = nodes_here // nc
    yrep = ("y",) + REP
    fours = [
        [((y + zh * nc + c) % ny) * nrep + zh * nc + c for zh in range(nzh)]
        for y in range(ny)
        for c in range(nc)
    ]
    pairs = []
    for y in range(ny):
        for zh in range(nzh):
            here, there = y * nrep + zh * nc, ((y + 1) % ny) * nrep + zh * nc + 1
            pairs += [(here, there), (there, here)]
    cores = [(0, 1), (1, 0)]
    scalars = [block_rows[0, 0].T, block_cols[0, 0].T]

    def place(flag):
        return jnp.stack([q_id, c_id, flag]).astype(jnp.int32)

    width = features.shape[1]
    part = w_first.shape[1] // nc
    bands = part // classes
    used = bands * width + part
    each = -(-(used + 3) // nq)
    each = -(-each // 16) * 16
    plain = place(jnp.int32(0))
    diagonal = place((rep_id == 0).astype(jnp.int32))
    from_same = lax.broadcasted_iota(jnp.int32, (nq, 1, classes), 0) >= q_id
    loss_row = lax.broadcasted_iota(jnp.int32, (each, classes), 0) - (used - q_id * each)
    labels_half = lax.dynamic_slice_in_dim(labels, c_id * half, half, 0)

    def in_terms(value):
        high = value.astype(BF)
        middle = (value - high.astype(F32)).astype(BF)
        low = (value - high.astype(F32) - middle.astype(F32)).astype(BF)
        return high, middle, low

    def summed(parts):
        sums = jnp.sum(parts.astype(F32), axis=0)
        at = used % each
        terms = in_terms(jnp.sum(sums[at : at + 3], axis=0, keepdims=True))
        sums = sums.astype(BF)
        for k, term in enumerate(terms):
            sums = jnp.where(loss_row == k, term, sums)
        return sums


    def to_all(value, count):
        return jnp.broadcast_to(value[None], (count,) + value.shape)

    def whole(mine, other):
        return jnp.where(
            c_id == 0,
            jnp.concatenate([mine, other], axis=-2),
            jnp.concatenate([other, mine], axis=-2),
        )

    def reduced(mine, away, *ahead):
        parts = (mine + lax.ppermute(away, yrep, pairs).astype(F32)).astype(BF)
        parts = lax.all_to_all(parts, "q", 0, 0, tiled=True).astype(F32)
        before = jnp.sum(jnp.where(from_same, 0.0, parts), axis=0).astype(BF)
        moved = lax.ppermute(before, "y", [((i + 1) % ny, i) for i in range(ny)])
        total = jnp.sum(jnp.where(from_same, parts, 0.0), axis=0) + moved.astype(F32)
        total, *ahead = lax.optimization_barrier((total.astype(BF), *ahead))
        group = lax.all_to_all(
            to_all(total, nzh), yrep, 0, 0, axis_index_groups=fours, tiled=True
        )
        return ((1.0 - ALPHA) * jnp.sum(group.astype(F32), axis=0)).astype(BF), *ahead

    def gathered(here):
        before = lax.ppermute(here, "y", [(i, (i + 1) % ny) for i in range(ny)])
        near = jnp.where(from_same, here[None], before[None])
        near = lax.all_to_all(near, "q", 0, 0, tiled=True)
        return near, lax.ppermute(near, yrep, pairs)

    slots_here = [((steps, half, classes), F32), ((steps, half, classes), BF)]
    sum_here = pltpu.VMEM((nodes_here, classes), F32)
    plain, diagonal, from_same = lax.optimization_barrier((plain, diagonal, from_same))
    operands = (tiles, features, w_first, w_second)
    hidden_shape = (nodes_here, w_first.shape[1])
    mine, away, tiles, hidden, base = call(
        first_kernel,
        slots_here + [(tiles.shape, BF), (hidden_shape, BF), ((nodes_here, classes), BF)],
        [diagonal],
        [],
        [pltpu.VMEM(v.shape, BF) for v in operands[1:]]
        + [pltpu.VMEM(hidden_shape, BF)]
        + [pltpu.SMEM(v.shape, jnp.int32) for v in scalars]
        + [pltpu.SemaphoreType.DMA((7,))],
        [*scalars, *operands],
        (3,),
        interpret=interpret,
    )
    base_half = lax.dynamic_slice_in_dim(base, c_id * half, half, 0)
    current, base_half, labels_half, loss_row = reduced(
        mine, away, base_half, labels_half, loss_row
    )
    near, far = gathered(current)
    mine, away = call(
        gather_kernel,
        [((half, classes), F32), ((half, classes), BF)],
        [plain] + scalars,
        [tiles, near, far],
        [sum_here],
        interpret=interpret,
    )
    chip = (mine + lax.ppermute(away, "c", cores).astype(F32)).astype(BF)
    chips = lax.all_to_all(to_all(chip, nzh), "zh", 0, 0, tiled=True)
    mixed = (1.0 - ALPHA) * jnp.sum(chips.astype(F32), axis=0) + ALPHA * base_half.astype(F32)
    chosen = labels_half[:, None] == jnp.arange(classes, dtype=jnp.int32)[None, :]
    top = jnp.max(mixed, axis=1, keepdims=True)
    grown = jnp.exp(mixed - top)
    mass = jnp.sum(grown, axis=1, keepdims=True)
    ce_rows = jnp.where(chosen, jnp.log(mass) + top - mixed, 0.0)
    ce_sum = jnp.sum(ce_rows, axis=0, keepdims=True)
    ce_terms = in_terms(jnp.where(lax.axis_index("zh") == 0, ce_sum, 0.0))
    grad_out = (grown / mass - chosen.astype(F32)) * (1.0 / math.sqrt(nodes))
    both, ce_terms = lax.optimization_barrier(
        (jnp.stack([grad_out.astype(BF), mixed.astype(BF)]), ce_terms)
    )
    both = whole(both, lax.ppermute(both, "c", cores))
    moving, logits = both[0], both[1]

    mine, away = call(
        scatter_kernel, slots_here, [plain] + scalars, [tiles, moving], interpret=interpret
    )
    (current,) = reduced(mine, away)
    near, far = gathered(current)
    (grad_b,) = call(
        last_kernel,
        [((nodes_here, classes), BF)],
        [diagonal] + scalars,
        [tiles, near, far, moving],
        [sum_here],
        interpret=interpret,
    )

    def weight_rows(core, grad_b):
        hidden_part = lax.dynamic_slice_in_dim(hidden, core * part, part, 1)
        second_part = lax.dynamic_slice_in_dim(w_second, core * part, part, 0)
        back = lax.dot_general(
            grad_b, second_part, (((1,), (1,)), ((), ())), preferred_element_type=F32
        )
        grad_hidden = jnp.where(hidden_part > 0, back, 0.0).astype(BF)
        first = lax.dot_general(
            features, grad_hidden, (((0,), (0,)), ((), ())), preferred_element_type=F32
        )
        second = lax.dot_general(
            hidden_part, grad_b, (((0,), (0,)), ((), ())), preferred_element_type=F32
        )
        bands_here = [first[:, k * classes : (k + 1) * classes] for k in range(bands)]
        return jnp.concatenate(bands_here + [second])

    away, grad_b = lax.optimization_barrier((weight_rows(1 - c_id, grad_b).astype(BF), grad_b))
    away = lax.ppermute(away, "c", cores)
    sums = (weight_rows(c_id, grad_b) + away.astype(F32)).astype(BF)
    sums = jnp.concatenate(
        [sums, *ce_terms, jnp.zeros((each * nq - used - 3, classes), BF)]
    ).reshape(nq, each, classes)
    sums = summed(lax.all_to_all(sums, "q", 0, 0, tiled=True))
    sums = summed(lax.all_to_all(to_all(sums, nzh), "zh", 0, 0, tiled=True))
    sums = summed(lax.all_to_all(to_all(sums, ny), "y", 0, 0, tiled=True))
    sums = lax.all_to_all(to_all(sums, nq), "q", 0, 0, tiled=True).reshape(nq * each, classes)
    other = lax.ppermute(sums, "c", cores)
    first_core = jnp.where(c_id == 0, sums, other).astype(F32)
    second_core = jnp.where(c_id == 0, other, sums).astype(F32)
    grad_first = jnp.concatenate(
        [v[k * width : (k + 1) * width] for v in (first_core, second_core) for k in range(bands)],
        axis=1,
    )
    grad_second = jnp.concatenate([v[bands * width : used] for v in (first_core, second_core)])
    loss = jnp.sum(first_core[used : used + 3] + second_core[used : used + 3]) / nodes
    return (logits, grad_first, grad_second, loss)


def solution(mesh, interpret=False):
    nblk, nrep = mesh.devices.shape
    cores = 2
    fine = Mesh(
        mesh.devices.reshape(nrep, nblk // nrep, nrep // cores, cores), ("y", "q", "zh", "c")
    )
    in_specs = (
        P(BLK, None),
        P(BLK),
        P(),
        P(),
        P(BLK, REP, None, None),
        P(BLK, REP, None, None),
        P(BLK, REP, None, None, None, None),
    )
    out_specs = (P(BLK, None), P(), P(), P())
    return jax.shard_map(
        functools.partial(on_device, interpret),
        mesh=fine,
        in_specs=in_specs,
        out_specs=out_specs,
        check_vma=False,
    )
```
